256 devices in a mesh: ctx: 16 (over z, core), tp: 16 (over y, x).
Axes of the slice: x: 4, y: 4, z: 8, core: 2. Of those that a mesh axis runs over, the one named last changes fastest.
Arguments:
- queries: bfloat16 [32768, 4096], P(('ctx', 'tp')), may hold values from -6 to 6, as said below
- keys: bfloat16 [32768, 2048], P(('ctx', 'tp')), may hold values from -9 to 9, as said below
- values: bfloat16 [32768, 2048], P(('ctx', 'tp')), may hold values from -5 to 5
- output_gradient: bfloat16 [32768, 4096], P(('ctx', 'tp')), may hold values from -5 to 5
Outputs:
- attn_out: bfloat16 [32768, 4096], P(('ctx', 'tp'))
- grad_q: bfloat16 [32768, 4096], P(('ctx', 'tp'))
- grad_k: bfloat16 [32768, 2048], P(('ctx', 'tp'))
- grad_v: bfloat16 [32768, 2048], P(('ctx', 'tp'))
The draws below stay inside these ranges and needn't reach their ends.
Inputs may be any that keep to these rules, and one draw needn't show every extreme that they name: queries are real-valued. keys are real-valued.
All inputs are finite; a program needn't handle non-finite values.
Results may differ from the reference program's by a relative error of at most 0.023.
Values may be sent and summed in bfloat16 or wider, within the bound.
A program may use at most 128 MiB of HBM per device.

```python
import jax
import jax.numpy as jnp
from jax import lax

HEAD_SIZE = 128
QUERY_GROUP = 2
WINDOW_LENGTH = 1024
QSCALE = 168
BLOCK = 512
KEY_VALUE_HEADS = 16
HQ = 32
SEQUENCE_TOKENS = 32768


def draw_queries(key, part):
    lowest_key_index = jax.random.fold_in(key, 1)
    final_output = jnp.clip(jax.random.normal(lowest_key_index, (SEQUENCE_TOKENS, HQ * HEAD_SIZE), jnp.float32), -3.0, 3.0)
    return final_output.astype(jnp.bfloat16)


def draw_keys(key, part):
    lowest_key_index = jax.random.fold_in(key, 2)
    spread_heads = jnp.exp(jax.random.uniform(jax.random.fold_in(key, 3), (SEQUENCE_TOKENS, 1), jnp.float32, jnp.log(0.3), jnp.log(3.0)))
    final_output = jnp.clip(jax.random.normal(lowest_key_index, (SEQUENCE_TOKENS, KEY_VALUE_HEADS * HEAD_SIZE), jnp.float32), -3.0, 3.0) * spread_heads
    return final_output.astype(jnp.bfloat16)


def level_of(rng, extent, cuts, smallest, high):
    loudness = 1.0
    for axis_at, blocks in cuts:
        draws = jax.random.uniform(jax.random.fold_in(jax.random.fold_in(rng, 6), axis_at), (blocks,), jnp.float32, smallest / len(cuts), high / len(cuts))
        loudness = loudness * jnp.repeat(jnp.exp(draws), extent[axis_at] // blocks).reshape((-1,) + (1,) * (len(extent) - 1 - axis_at))
    return loudness


def noise(rng, extent, deviation, limit, cuts=(), kind=jnp.bfloat16):
    result = deviation * jax.random.normal(rng, extent, jnp.float32)
    if cuts:
        result = result * level_of(rng, extent, cuts, -0.22, 0.18)
    return jnp.clip(result, -limit, limit).astype(kind)


def setup_inputs(seed: int = 0) -> dict:
    key_list = jax.random.split(jax.random.key(seed), 5)
    return {
        "queries": draw_queries(jax.random.fold_in(key_list[4], 71), 0),
        "keys": draw_keys(jax.random.fold_in(key_list[4], 71), 0),
        "values": noise(key_list[2], (SEQUENCE_TOKENS, KEY_VALUE_HEADS * HEAD_SIZE), 1.0, 5.0, ((0, 256),)),
        "output_gradient": noise(key_list[3], (SEQUENCE_TOKENS, HQ * HEAD_SIZE), 1.0, 5.0, ((0, 256),)),
    }


def band_mask(start, first):
    offsets = jnp.arange(BLOCK + WINDOW_LENGTH)[None, :] - jnp.arange(BLOCK)[:, None]
    inside = (offsets >= 1) & (offsets <= WINDOW_LENGTH)
    present = (start + jnp.arange(BLOCK + WINDOW_LENGTH) >= WINDOW_LENGTH) | first
    return (inside & present[None, :])[None]


def softmax_rows(logits, allowed):
    masked = jnp.where(allowed, logits, -jnp.inf)
    highest = jnp.max(masked, axis=-1, keepdims=True)
    raised = jnp.where(allowed, jnp.exp(masked - highest), 0.0)
    totals = jnp.sum(raised, axis=-1, keepdims=True)
    return raised / totals, highest, totals


def reference(queries, keys, values, output_gradient):
    scale = QSCALE ** -0.5
    window_span = BLOCK + WINDOW_LENGTH
    head_count = queries.reshape(SEQUENCE_TOKENS, KEY_VALUE_HEADS, QUERY_GROUP, HEAD_SIZE)
    gradient_tuple = output_gradient.reshape(SEQUENCE_TOKENS, KEY_VALUE_HEADS, QUERY_GROUP, HEAD_SIZE)
    padding_rows = jnp.zeros((WINDOW_LENGTH, KEY_VALUE_HEADS, HEAD_SIZE), jnp.bfloat16)
    key_extended = jnp.concatenate([padding_rows, keys.reshape(SEQUENCE_TOKENS, KEY_VALUE_HEADS, HEAD_SIZE)], 0)
    value_extended = jnp.concatenate([padding_rows, values.reshape(SEQUENCE_TOKENS, KEY_VALUE_HEADS, HEAD_SIZE)], 0)
    start_indices = jnp.arange(SEQUENCE_TOKENS // BLOCK, dtype=jnp.int32) * BLOCK

    def forward_pass(start):
        query_block = lax.dynamic_slice_in_dim(head_count, start, BLOCK, 0)
        key_block = lax.dynamic_slice_in_dim(key_extended, start, window_span, 0)
        value_block = lax.dynamic_slice_in_dim(value_extended, start, window_span, 0)
        allowed = band_mask(start, False)
        pieces = []
        for member in range(QUERY_GROUP):
            logits = jnp.einsum('bhd,lhd->hbl', query_block[:, :, member].astype(jnp.float32), key_block.astype(jnp.float32)) * scale
            probs = softmax_rows(logits, allowed)[0].astype(jnp.bfloat16)
            pieces.append(jnp.einsum('hbl,lhd->bhd', probs.astype(jnp.float32), value_block.astype(jnp.float32)))
        return jnp.stack(pieces, 2).astype(jnp.bfloat16)

    attended_output = lax.map(forward_pass, start_indices).reshape(SEQUENCE_TOKENS, KEY_VALUE_HEADS, QUERY_GROUP, HEAD_SIZE)
    delta = jnp.sum(gradient_tuple.astype(jnp.float32) * attended_output.astype(jnp.float32), -1)

    def backward(number, carry):
        key_gradient, value_gradient, query_grad = carry
        start = number * BLOCK
        query_block = lax.dynamic_slice_in_dim(head_count, start, BLOCK, 0)
        grad_block = lax.dynamic_slice_in_dim(gradient_tuple, start, BLOCK, 0)
        delta_block = lax.dynamic_slice_in_dim(delta, start, BLOCK, 0)
        key_block = lax.dynamic_slice_in_dim(key_extended, start, window_span, 0)
        value_block = lax.dynamic_slice_in_dim(value_extended, start, window_span, 0)
        allowed = band_mask(start, False)
        key_portion = jnp.zeros((window_span, KEY_VALUE_HEADS, HEAD_SIZE), jnp.float32)
        value_portion = jnp.zeros((window_span, KEY_VALUE_HEADS, HEAD_SIZE), jnp.float32)
        pieces = []
        for member in range(QUERY_GROUP):
            query_one = query_block[:, :, member].astype(jnp.float32)
            grad_one = grad_block[:, :, member].astype(jnp.float32)
            logits = jnp.einsum('bhd,lhd->hbl', query_one, key_block.astype(jnp.float32)) * scale
            probs = softmax_rows(logits, allowed)[0]
            probs_low = probs.astype(jnp.bfloat16).astype(jnp.float32)
            value_portion = value_portion + jnp.einsum('hbl,bhd->lhd', probs_low, grad_one)
            dprobs = jnp.einsum('bhd,lhd->hbl', grad_one, value_block.astype(jnp.float32))
            dlogits = (probs * (dprobs - delta_block[:, :, member].T[:, :, None])).astype(jnp.bfloat16).astype(jnp.float32)
            pieces.append((jnp.einsum('hbl,lhd->bhd', dlogits, key_block.astype(jnp.float32)) * scale).astype(jnp.bfloat16))
            key_portion = key_portion + jnp.einsum('hbl,bhd->lhd', dlogits, query_one) * scale
        query_grad = lax.dynamic_update_slice_in_dim(query_grad, jnp.stack(pieces, 2), start, 0)
        key_gradient = lax.dynamic_update_slice_in_dim(key_gradient, lax.dynamic_slice_in_dim(key_gradient, start, window_span, 0) + key_portion, start, 0)
        value_gradient = lax.dynamic_update_slice_in_dim(value_gradient, lax.dynamic_slice_in_dim(value_gradient, start, window_span, 0) + value_portion, start, 0)
        return key_gradient, value_gradient, query_grad

    starting_value = (jnp.zeros((SEQUENCE_TOKENS + WINDOW_LENGTH, KEY_VALUE_HEADS, HEAD_SIZE), jnp.float32), jnp.zeros((SEQUENCE_TOKENS + WINDOW_LENGTH, KEY_VALUE_HEADS, HEAD_SIZE), jnp.float32), jnp.zeros((SEQUENCE_TOKENS, KEY_VALUE_HEADS, QUERY_GROUP, HEAD_SIZE), jnp.bfloat16))
    key_gradient, value_gradient, query_grad = lax.fori_loop(0, SEQUENCE_TOKENS // BLOCK, backward, starting_value)
    return (attended_output.reshape(SEQUENCE_TOKENS, HQ * HEAD_SIZE), query_grad.reshape(SEQUENCE_TOKENS, HQ * HEAD_SIZE),
            key_gradient[WINDOW_LENGTH:].astype(jnp.bfloat16).reshape(SEQUENCE_TOKENS, KEY_VALUE_HEADS * HEAD_SIZE),
            value_gradient[WINDOW_LENGTH:].astype(jnp.bfloat16).reshape(SEQUENCE_TOKENS, KEY_VALUE_HEADS * HEAD_SIZE))
```

```python
import functools
import math

import jax
import jax.numpy as jnp
from jax import lax
from jax.experimental import pallas as pl
from jax.experimental.pallas import tpu as pltpu
from jax.sharding import PartitionSpec as P

HEAD = 128
GROUP = 2
WINDOW = 1024
QSCALE = 168
SCALE = QSCALE ** (-0.5)
EXP_SCALE = SCALE * math.log2(math.e)
FAR = 1e30
MESH = pl.DeviceIdType.MESH
F32 = jnp.float32
BF16 = jnp.bfloat16


def attention_kernel(
    tp, ctx, rows,
    q_in, k_in, v_in, g_in,
    o_out, dq_out, dk_out, dv_out,
    qs, kx, vx, gs, kt, vt, scores, ex, ot, rl, acc_k, acc_v, dlog,
    o_buf, dq_buf, dk_buf, dv_buf, halo_out, halo_in,
    in_send, in_recv, out_send, out_recv, halo_send, halo_recv, own_in, own_out,
):
    me = lax.axis_index("tp")
    place = lax.axis_index("ctx")
    ahead, behind = lax.rem(place + 1, ctx), lax.rem(place + ctx - 1, ctx)
    shard = rows * tp
    blocks = shard // rows
    span = WINDOW + rows
    halo_blocks = WINDOW // rows
    wide = GROUP * HEAD

    def at(i, size=rows):
        return pl.ds(pl.multiple_of(i * rows, rows), size)

    def columns(i, width):
        return pl.ds(pl.multiple_of(i * width, width), width)

    barrier = pltpu.get_barrier_semaphore()
    for n in range(1, tp):
        pl.semaphore_signal(barrier, inc=1, device_id={"tp": lax.rem(me + n, tp)}, device_id_type=MESH)
    pl.semaphore_signal(barrier, inc=1, device_id={"ctx": ahead}, device_id_type=MESH)
    pl.semaphore_signal(barrier, inc=1, device_id={"ctx": behind}, device_id_type=MESH)
    pl.semaphore_wait(barrier, tp + 1)

    incoming = (
        (k_in, kx, HEAD, halo_blocks),
        (v_in, vx, HEAD, halo_blocks),
        (q_in, qs, wide, 0),
        (g_in, gs, wide, 0),
    )

    def in_copy(i, owner, peer):
        source, target, width, first = incoming[i]
        return pltpu.make_async_remote_copy(
            src_ref=source.at[:, columns(peer, width)],
            dst_ref=target.at[at(first + owner), :],
            send_sem=in_send.at[i, peer],
            recv_sem=in_recv.at[i, owner],
            device_id={"tp": peer},
            device_id_type=MESH,
        )

    def own_copy(i):
        source, target, width, first = incoming[i]
        return pltpu.make_async_copy(
            source.at[:, columns(me, width)], target.at[at(first + me), :], own_in.at[i]
        )

    for i in range(4):
        def send(n, _, i=i):
            in_copy(i, me, lax.rem(me + n, tp)).start()
            return 0
        lax.fori_loop(1, tp, send, 0)
        own_copy(i).start()

    def arrived(i):
        def wait(n, _):
            in_copy(i, lax.rem(me + n, tp), me).wait_recv()
            return 0
        lax.fori_loop(1, tp, wait, 0)
        own_copy(i).wait()

    acc_k[...] = jnp.zeros_like(acc_k)
    acc_v[...] = jnp.zeros_like(acc_v)

    def halo_copy(i, source, target, where):
        return pltpu.make_async_remote_copy(
            src_ref=source, dst_ref=target, send_sem=halo_send.at[i], recv_sem=halo_recv.at[i],
            device_id={"ctx": where}, device_id_type=MESH,
        )

    halo_k = halo_copy(0, kx.at[pl.ds(shard, WINDOW), :], kx.at[pl.ds(0, WINDOW), :], ahead)
    halo_v = halo_copy(1, vx.at[pl.ds(shard, WINDOW), :], vx.at[pl.ds(0, WINDOW), :], ahead)
    halo_dk = halo_copy(2, halo_out.at[0], halo_in.at[0], behind)
    halo_dv = halo_copy(3, halo_out.at[1], halo_in.at[1], behind)

    def turn(source, target, first, count):
        def step(n, _):
            target[:, at(first + n)] = source[at(first + n), :].T
            return 0
        lax.fori_loop(0, count, step, 0)

    arrived(0)
    halo_k.start()
    turn(kx, kt, halo_blocks, blocks)
    arrived(1)
    halo_v.start()
    turn(vx, vt, halo_blocks, blocks)
    arrived(2)

    row_of = lax.broadcasted_iota(jnp.int32, (rows, wide), 0)
    col_of = lax.rem(lax.broadcasted_iota(jnp.int32, (rows, wide), 1), rows)
    causal = row_of <= col_of

    outgoing = (
        (o_buf, o_out, wide), (dq_buf, dq_out, wide), (dk_buf, dk_out, HEAD), (dv_buf, dv_out, HEAD),
    )

    def out_copy(i, owner, peer):
        source, target, width = outgoing[i]
        return pltpu.make_async_remote_copy(
            src_ref=source.at[peer],
            dst_ref=target.at[:, columns(owner, width)],
            send_sem=out_send.at[i, peer],
            recv_sem=out_recv.at[i, owner],
            device_id={"tp": peer},
            device_id_type=MESH,
        )

    def keep_copy(i):
        source, target, width = outgoing[i]
        return pltpu.make_async_copy(source.at[me], target.at[:, columns(me, width)], own_out.at[i])

    def deliver(i, b):
        @pl.when(b != me)
        def _():
            out_copy(i, me, b).start()

        @pl.when(b == me)
        def _():
            keep_copy(i).start()

    def stacked(ref, b):
        block = ref[at(b), :]
        return jnp.concatenate([block[:, :HEAD], block[:, HEAD:]], axis=0)

    def unstacked(t):
        return jnp.concatenate([t[:, :rows].T, t[:, rows:].T], axis=1)

    def fold(op, x):
        return op(x.reshape(rows // 8, 8, wide), axis=0)

    nt = (((1,), (1,)), ((), ()))
    chunks = WINDOW // rows

    def forward(b):
        query = stacked(qs, b)
        scores[...] = lax.dot_general(kx[at(b, span), :], query, nt, preferred_element_type=F32)
        present = [jnp.logical_or(place > 0, j + b >= halo_blocks) for j in range(chunks)]
        diagonal = scores[pl.ds(WINDOW, rows), :]
        scores[pl.ds(0, rows), :] = jnp.where(
            causal, diagonal, jnp.where(present[0], scores[pl.ds(0, rows), :], -FAR)
        )
        top = fold(jnp.max, scores[pl.ds(0, rows), :])
        for j in range(1, chunks):
            part = fold(jnp.max, scores[pl.ds(j * rows, rows), :])
            top = jnp.maximum(top, jnp.where(present[j], part, -FAR))
        shift = jnp.max(top, axis=0, keepdims=True) * EXP_SCALE
        total = jnp.zeros((8, wide), F32)
        for j in range(chunks):
            by = shift if j == 0 else jnp.where(present[j], shift, FAR)
            e = jnp.exp2(scores[pl.ds(j * rows, rows), :] * EXP_SCALE - by)
            total = total + fold(jnp.sum, e)
            if j == 0:
                ex[b, pl.ds(0, rows), :] = jnp.where(causal, 0.0, e).astype(BF16)
                ex[b, pl.ds(WINDOW, rows), :] = jnp.where(causal, e, 0.0).astype(BF16)
            else:
                ex[b, pl.ds(j * rows, rows), :] = e.astype(BF16)
        inverse = 1.0 / jnp.sum(total, axis=0, keepdims=True)
        rl[b] = inverse
        out = jnp.dot(vt[:, at(b, span)], ex[b], preferred_element_type=F32) * inverse
        out = out.astype(BF16)
        ot[b] = out
        o_buf[b] = unstacked(out)
        deliver(0, b)

    def backward(b):
        query = stacked(qs, b)
        grad_t = (stacked(gs, b).astype(F32).T * rl[b]).astype(BF16)
        delta = jnp.sum(grad_t.astype(F32) * ot[b].astype(F32), axis=0, keepdims=True)
        grad = grad_t.T
        scores[...] = jnp.dot(vx[at(b, span), :], grad_t, preferred_element_type=F32)
        first = jnp.where(causal, scores[pl.ds(WINDOW, rows), :], scores[pl.ds(0, rows), :])
        e = ex[b, pl.ds(0, rows), :].astype(F32) + ex[b, pl.ds(WINDOW, rows), :].astype(F32)
        d = e * (first - delta)
        dlog[pl.ds(0, rows), :] = jnp.where(causal, 0.0, d).astype(BF16)
        dlog[pl.ds(WINDOW, rows), :] = jnp.where(causal, d, 0.0).astype(BF16)
        for j in range(1, chunks):
            part = pl.ds(j * rows, rows)
            dlog[part, :] = (ex[b, part, :].astype(F32) * (scores[part, :] - delta)).astype(BF16)
        window = at(b, span)
        acc_v[window, :] += jnp.dot(ex[b], grad, preferred_element_type=F32)
        acc_k[window, :] += jnp.dot(dlog[...], query, preferred_element_type=F32)
        dq_t = jnp.dot(kt[:, window], dlog[...], preferred_element_type=F32) * SCALE
        dq_buf[b] = unstacked(dq_t.astype(BF16))
        deliver(1, b)

    half = blocks // 2

    def over(base, work):
        def step(n, _):
            work(base + lax.rem(n + me, half))
            return 0
        lax.fori_loop(0, half, step, 0)

    over(half, forward)
    halo_k.wait_recv()
    turn(kx, kt, 0, halo_blocks)
    halo_v.wait_recv()
    turn(vx, vt, 0, halo_blocks)
    over(0, forward)

    arrived(3)
    over(0, backward)

    def pack(n, _):
        halo_out[0, at(n), :] = (acc_k[at(n), :] * SCALE).astype(BF16)
        halo_out[1, at(n), :] = acc_v[at(n), :].astype(BF16)
        return 0
    lax.fori_loop(0, halo_blocks, pack, 0)
    halo_dk.start()
    halo_dv.start()
    over(half, backward)

    def finish_early(b):
        dk_buf[b] = (acc_k[at(b + halo_blocks), :] * SCALE).astype(BF16)
        dv_buf[b] = acc_v[at(b + halo_blocks), :].astype(BF16)
        deliver(2, b)
        deliver(3, b)

    def finish_late(b):
        more = at(b - (blocks - halo_blocks))
        dk_buf[b] = (acc_k[at(b + halo_blocks), :] * SCALE + halo_in[0, more, :].astype(F32)).astype(BF16)
        dv_buf[b] = (acc_v[at(b + halo_blocks), :] + halo_in[1, more, :].astype(F32)).astype(BF16)
        deliver(2, b)
        deliver(3, b)

    over(0, finish_early)
    halo_dk.wait_recv()
    halo_dv.wait_recv()
    over(half, finish_late)

    for i in range(4):
        def wait(n, _, i=i):
            peer = lax.rem(me + n, tp)
            in_copy(i, me, peer).wait_send()
            out_copy(i, me, peer).wait_send()
            out_copy(i, peer, me).wait_recv()
            return 0
        lax.fori_loop(1, tp, wait, 0)
        keep_copy(i).wait()
    for copy in (halo_k, halo_v, halo_dk, halo_dv):
        copy.wait_send()


def solution(mesh):
    tp, ctx = mesh.shape["tp"], mesh.shape["ctx"]

    def on_device(queries, keys, values, output_gradient):
        rows = queries.shape[0]
        shard = rows * tp
        wide = GROUP * HEAD
        span = WINDOW + rows
        hbm = pl.BlockSpec(memory_space=pl.ANY)
        dma = pltpu.SemaphoreType.DMA
        return pl.pallas_call(
            functools.partial(attention_kernel, tp, ctx, rows),
            out_shape=[
                jax.ShapeDtypeStruct(queries.shape, BF16),
                jax.ShapeDtypeStruct(queries.shape, BF16),
                jax.ShapeDtypeStruct(keys.shape, BF16),
                jax.ShapeDtypeStruct(keys.shape, BF16),
            ],
            in_specs=[hbm] * 4,
            out_specs=[hbm] * 4,
            scratch_shapes=[
                pltpu.VMEM((shard, wide), BF16),
                pltpu.VMEM((WINDOW + shard, HEAD), BF16),
                pltpu.VMEM((WINDOW + shard, HEAD), BF16),
                pltpu.VMEM((shard, wide), BF16),
                pltpu.VMEM((HEAD, WINDOW + shard), BF16),
                pltpu.VMEM((HEAD, WINDOW + shard), BF16),
                pltpu.VMEM((span, wide), F32),
                pltpu.VMEM((tp, span, wide), BF16),
                pltpu.VMEM((tp, HEAD, wide), BF16),
                pltpu.VMEM((tp, 1, wide), F32),
                pltpu.VMEM((WINDOW + shard, HEAD), F32),
                pltpu.VMEM((WINDOW + shard, HEAD), F32),
                pltpu.VMEM((span, wide), BF16),
                pltpu.VMEM((tp, rows, wide), BF16),
                pltpu.VMEM((tp, rows, wide), BF16),
                pltpu.VMEM((tp, rows, HEAD), BF16),
                pltpu.VMEM((tp, rows, HEAD), BF16),
                pltpu.VMEM((2, WINDOW, HEAD), BF16),
                pltpu.VMEM((2, WINDOW, HEAD), BF16),
                dma((4, tp)), dma((4, tp)), dma((4, tp)), dma((4, tp)),
                dma((4,)), dma((4,)), dma((4,)), dma((4,)),
            ],
            compiler_params=pltpu.CompilerParams(
                collective_id=0, has_side_effects=True, vmem_limit_bytes=60 << 20
            ),
        )(queries, keys, values, output_gradient)

    spec = P(("ctx", "tp"), None)
    return jax.shard_map(
        on_device, mesh=mesh, in_specs=(spec,) * 4, out_specs=(spec,) * 4, check_vma=False
    )
```

```python
import functools
import math

import jax
import jax.numpy as jnp
from jax import lax
from jax.experimental import pallas as pl
from jax.experimental.pallas import tpu as pltpu
from jax.sharding import PartitionSpec as P

HEAD = 128
GROUP = 2
WINDOW = 1024
QSCALE = 168
SCALE = QSCALE ** (-0.5)
EXP_SCALE = SCALE * math.log2(math.e)
FAR = 1e30
FIRST = (0, 1, 2)
MESH = pl.DeviceIdType.MESH
F32 = jnp.float32
BF16 = jnp.bfloat16


def attention_kernel(
    tp, ctx, rows,
    q_in, k_in, v_in, g_in,
    o_out, dq_out, dk_out, dv_out,
    qs, kx, vx, gs, kt, vt, scores, ex, ot, rl, acc_k, acc_v, dlog,
    o_buf, dq_buf, dk_buf, dv_buf, halo_out, halo_in,
    in_send, in_recv, out_send, out_recv, halo_send, halo_recv, own_in, own_out,
):
    me = lax.axis_index("tp")
    place = lax.axis_index("ctx")
    ahead, behind = lax.rem(place + 1, ctx), lax.rem(place + ctx - 1, ctx)
    shard = rows * tp
    blocks = shard // rows
    span = WINDOW + rows
    halo_blocks = WINDOW // rows
    wide = GROUP * HEAD

    def at(i, size=rows):
        return pl.ds(pl.multiple_of(i * rows, rows), size)

    def columns(i, width):
        return pl.ds(pl.multiple_of(i * width, width), width)

    barrier = pltpu.get_barrier_semaphore()
    for n in range(1, tp):
        pl.semaphore_signal(barrier, inc=1, device_id={"tp": lax.rem(me + n, tp)}, device_id_type=MESH)
    pl.semaphore_signal(barrier, inc=1, device_id={"ctx": ahead}, device_id_type=MESH)
    pl.semaphore_signal(barrier, inc=1, device_id={"ctx": behind}, device_id_type=MESH)
    pl.semaphore_wait(barrier, tp + 1)

    incoming = (
        (k_in, kx, HEAD, halo_blocks),
        (v_in, vx, HEAD, halo_blocks),
        (q_in, qs, wide, 0),
        (g_in, gs, wide, 0),
    )

    def in_copy(i, owner, peer):
        source, target, width, first = incoming[i]
        return pltpu.make_async_remote_copy(
            src_ref=source.at[:, columns(peer, width)],
            dst_ref=target.at[at(first + owner), :],
            send_sem=in_send.at[i, peer],
            recv_sem=in_recv.at[i, owner],
            device_id={"tp": peer},
            device_id_type=MESH,
        )

    def own_copy(i):
        source, target, width, first = incoming[i]
        return pltpu.make_async_copy(
            source.at[:, columns(me, width)], target.at[at(first + me), :], own_in.at[i]
        )

    side = math.isqrt(tp)
    x, y = lax.rem(me, side), me // side
    core = lax.rem(place, 2)

    def partner(dx, dy):
        dx = jnp.where(core == 0, dx, side - dx)
        dy = jnp.where(core == 0, dy, side - dy)
        return lax.rem(y + dy, side) * side + lax.rem(x + dx, side)

    far = sorted(
        ((dx, dy) for dx in range(side) for dy in range(side) if dx or dy),
        key=lambda d: -(min(d[0], side - d[0]) + min(d[1], side - d[1])),
    )
    partners = [partner(dx, dy) for dx, dy in far]

    def send(i):
        for peer in partners:
            in_copy(i, me, peer).start()

    def sent(i):
        for peer in partners:
            in_copy(i, me, peer).wait_send()

    for i in FIRST:
        send(i)
    for i in range(4):
        own_copy(i).start()

    def arrived(i):
        def wait(n, _):
            in_copy(i, lax.rem(me + n, tp), me).wait_recv()
            return 0
        lax.fori_loop(1, tp, wait, 0)
        own_copy(i).wait()

    acc_k[...] = jnp.zeros_like(acc_k)
    acc_v[...] = jnp.zeros_like(acc_v)

    def halo_copy(i, source, target, where):
        return pltpu.make_async_remote_copy(
            src_ref=source, dst_ref=target, send_sem=halo_send.at[i], recv_sem=halo_recv.at[i],
            device_id={"ctx": where}, device_id_type=MESH,
        )

    halo_k = halo_copy(0, kx.at[pl.ds(shard, WINDOW), :], kx.at[pl.ds(0, WINDOW), :], ahead)
    halo_v = halo_copy(1, vx.at[pl.ds(shard, WINDOW), :], vx.at[pl.ds(0, WINDOW), :], ahead)
    halo_dk = halo_copy(2, halo_out.at[0], halo_in.at[0], behind)
    halo_dv = halo_copy(3, halo_out.at[1], halo_in.at[1], behind)

    def turn(source, target, first, count):
        def step(n, _):
            target[:, at(first + n)] = source[at(first + n), :].T
            return 0
        lax.fori_loop(0, count, step, 0)

    arrived(0)
    halo_k.start()
    turn(kx, kt, halo_blocks, blocks)
    arrived(1)
    halo_v.start()
    turn(vx, vt, halo_blocks, blocks)
    for i in FIRST:
        sent(i)
    for i in range(4):
        if i not in FIRST:
            send(i)
    halo_k.wait_recv()
    turn(kx, kt, 0, halo_blocks)
    halo_v.wait_recv()
    turn(vx, vt, 0, halo_blocks)
    arrived(2)

    row_of = lax.broadcasted_iota(jnp.int32, (rows, wide), 0)
    col_of = lax.rem(lax.broadcasted_iota(jnp.int32, (rows, wide), 1), rows)
    causal = row_of <= col_of

    outgoing = (
        (o_buf, o_out, wide), (dq_buf, dq_out, wide), (dk_buf, dk_out, HEAD), (dv_buf, dv_out, HEAD),
    )

    def out_copy(i, owner, peer):
        source, target, width = outgoing[i]
        return pltpu.make_async_remote_copy(
            src_ref=source.at[peer],
            dst_ref=target.at[:, columns(owner, width)],
            send_sem=out_send.at[i, peer],
            recv_sem=out_recv.at[i, owner],
            device_id={"tp": peer},
            device_id_type=MESH,
        )

    def keep_copy(i):
        source, target, width = outgoing[i]
        return pltpu.make_async_copy(source.at[me], target.at[:, columns(me, width)], own_out.at[i])

    def deliver(i, b):
        @pl.when(b != me)
        def _():
            out_copy(i, me, b).start()

        @pl.when(b == me)
        def _():
            keep_copy(i).start()

    def stacked(ref, b):
        block = ref[at(b), :]
        return jnp.concatenate([block[:, :HEAD], block[:, HEAD:]], axis=0)

    def unstacked(t):
        return jnp.concatenate([t[:, :rows].T, t[:, rows:].T], axis=1)

    def fold(op, x):
        return op(x.reshape(rows // 8, 8, wide), axis=0)

    nt = (((1,), (1,)), ((), ()))
    chunks = WINDOW // rows

    def forward(b):
        query = stacked(qs, b)
        scores[...] = lax.dot_general(kx[at(b, span), :], query, nt, preferred_element_type=F32)
        present = [jnp.logical_or(place > 0, j + b >= halo_blocks) for j in range(chunks)]
        diagonal = scores[pl.ds(WINDOW, rows), :]
        scores[pl.ds(0, rows), :] = jnp.where(
            causal, diagonal, jnp.where(present[0], scores[pl.ds(0, rows), :], -FAR)
        )
        top = fold(jnp.max, scores[pl.ds(0, rows), :])
        for j in range(1, chunks):
            part = fold(jnp.max, scores[pl.ds(j * rows, rows), :])
            top = jnp.maximum(top, jnp.where(present[j], part, -FAR))
        shift = jnp.max(top, axis=0, keepdims=True) * EXP_SCALE
        total = jnp.zeros((8, wide), F32)
        for j in range(chunks):
            by = shift if j == 0 else jnp.where(present[j], shift, FAR)
            e = jnp.exp2(scores[pl.ds(j * rows, rows), :] * EXP_SCALE - by)
            total = total + fold(jnp.sum, e)
            if j == 0:
                ex[b, pl.ds(0, rows), :] = jnp.where(causal, 0.0, e).astype(BF16)
                ex[b, pl.ds(WINDOW, rows), :] = jnp.where(causal, e, 0.0).astype(BF16)
            else:
                ex[b, pl.ds(j * rows, rows), :] = e.astype(BF16)
        inverse = 1.0 / jnp.sum(total, axis=0, keepdims=True)
        rl[b] = inverse
        out = jnp.dot(vt[:, at(b, span)], ex[b], preferred_element_type=F32) * inverse
        out = out.astype(BF16)
        ot[b] = out
        o_buf[b] = unstacked(out)
        deliver(0, b)

    def backward(b):
        query = stacked(qs, b)
        grad_t = (stacked(gs, b).astype(F32).T * rl[b]).astype(BF16)
        delta = jnp.sum(grad_t.astype(F32) * ot[b].astype(F32), axis=0, keepdims=True)
        grad = grad_t.T
        scores[...] = jnp.dot(vx[at(b, span), :], grad_t, preferred_element_type=F32)
        first = jnp.where(causal, scores[pl.ds(WINDOW, rows), :], scores[pl.ds(0, rows), :])
        e = ex[b, pl.ds(0, rows), :].astype(F32) + ex[b, pl.ds(WINDOW, rows), :].astype(F32)
        d = e * (first - delta)
        dlog[pl.ds(0, rows), :] = jnp.where(causal, 0.0, d).astype(BF16)
        dlog[pl.ds(WINDOW, rows), :] = jnp.where(causal, d, 0.0).astype(BF16)
        for j in range(1, chunks):
            part = pl.ds(j * rows, rows)
            dlog[part, :] = (ex[b, part, :].astype(F32) * (scores[part, :] - delta)).astype(BF16)
        window = at(b, span)
        acc_v[window, :] += jnp.dot(ex[b], grad, preferred_element_type=F32)
        acc_k[window, :] += jnp.dot(dlog[...], query, preferred_element_type=F32)
        dq_t = jnp.dot(kt[:, window], dlog[...], preferred_element_type=F32) * SCALE
        dq_buf[b] = unstacked(dq_t.astype(BF16))
        deliver(1, b)

    half = blocks // 2

    def over(base, count, work):
        def step(n, _):
            high = count // side
            dx = lax.rem(2 + lax.rem(n, side), side)
            dy = lax.rem(high // 2 + n // side, high)
            bx = lax.rem(x + jnp.where(core == 0, dx, side - dx), side)
            by = lax.rem(y + jnp.where(core == 0, dy, high - dy), high)
            work(base + by * side + bx)
            return 0
        lax.fori_loop(0, count, step, 0)

    over(0, blocks, forward)
    arrived(3)
    over(0, half, backward)

    def pack(n, _):
        halo_out[0, at(n), :] = (acc_k[at(n), :] * SCALE).astype(BF16)
        halo_out[1, at(n), :] = acc_v[at(n), :].astype(BF16)
        return 0
    lax.fori_loop(0, halo_blocks, pack, 0)
    halo_dk.start()
    halo_dv.start()
    over(half, half, backward)

    halo_dk.wait_recv()
    halo_dv.wait_recv()

    def finish(b):
        late = b - (blocks - halo_blocks)
        more = at(jnp.maximum(late, 0))
        weight = (late >= 0).astype(F32)
        own = at(b + halo_blocks)
        dk_buf[b] = (acc_k[own, :] * SCALE + weight * halo_in[0, more, :].astype(F32)).astype(BF16)
        deliver(2, b)
        dv_buf[b] = (acc_v[own, :] + weight * halo_in[1, more, :].astype(F32)).astype(BF16)
        deliver(3, b)

    over(0, blocks, finish)

    for i in range(4):
        def wait(n, _, i=i):
            peer = lax.rem(me + n, tp)
            out_copy(i, me, peer).wait_send()
            out_copy(i, peer, me).wait_recv()
            return 0
        lax.fori_loop(1, tp, wait, 0)
        keep_copy(i).wait()
    for i in range(4):
        if i not in FIRST:
            sent(i)
    for copy in (halo_k, halo_v, halo_dk, halo_dv):
        copy.wait_send()


def solution(mesh):
    tp, ctx = mesh.shape["tp"], mesh.shape["ctx"]

    def on_device(queries, keys, values, output_gradient):
        rows = queries.shape[0]
        shard = rows * tp
        wide = GROUP * HEAD
        span = WINDOW + rows
        hbm = pl.BlockSpec(memory_space=pl.ANY)
        vmem = pl.BlockSpec(memory_space=pltpu.VMEM)
        dma = pltpu.SemaphoreType.DMA
        results = pl.pallas_call(
            functools.partial(attention_kernel, tp, ctx, rows),
            out_shape=[pltpu.VMEM(a.shape, BF16) for a in (queries, queries, keys, keys)],
            in_specs=[hbm] * 4,
            out_specs=[vmem] * 4,
            scratch_shapes=[
                pltpu.VMEM((shard, wide), BF16),
                pltpu.VMEM((WINDOW + shard, HEAD), BF16),
                pltpu.VMEM((WINDOW + shard, HEAD), BF16),
                pltpu.VMEM((shard, wide), BF16),
                pltpu.VMEM((HEAD, WINDOW + shard), BF16),
                pltpu.VMEM((HEAD, WINDOW + shard), BF16),
                pltpu.VMEM((span, wide), F32),
                pltpu.VMEM((tp, span, wide), BF16),
                pltpu.VMEM((tp, HEAD, wide), BF16),
                pltpu.VMEM((tp, 1, wide), F32),
                pltpu.VMEM((WINDOW + shard, HEAD), F32),
                pltpu.VMEM((WINDOW + shard, HEAD), F32),
                pltpu.VMEM((span, wide), BF16),
                pltpu.VMEM((tp, rows, wide), BF16),
                pltpu.VMEM((tp, rows, wide), BF16),
                pltpu.VMEM((tp, rows, HEAD), BF16),
                pltpu.VMEM((tp, rows, HEAD), BF16),
                pltpu.VMEM((2, WINDOW, HEAD), BF16),
                pltpu.VMEM((2, WINDOW, HEAD), BF16),
                dma((4, tp)), dma((4, tp)), dma((4, tp)), dma((4, tp)),
                dma((4,)), dma((4,)), dma((4,)), dma((4,)),
            ],
            compiler_params=pltpu.CompilerParams(
                collective_id=0, has_side_effects=True, vmem_limit_bytes=60 << 20
            ),
        )(queries, keys, values, output_gradient)
        return results

    spec = P(("ctx", "tp"), None)
    return jax.shard_map(
        on_device, mesh=mesh, in_specs=(spec,) * 4, out_specs=(spec,) * 4, check_vma=False
    )
```

```python
import functools
import math

import jax
import jax.numpy as jnp
from jax import lax
from jax.experimental import pallas as pl
from jax.experimental.pallas import tpu as pltpu
from jax.sharding import PartitionSpec as P

HEAD = 128
GROUP = 2
WINDOW = 1024
QSCALE = 168
SCALE = QSCALE ** (-0.5)
EXP_SCALE = SCALE * math.log2(math.e)
FAR = 1e30
FIRST = (0, 1, 2)
EARLY = 10
MESH = pl.DeviceIdType.MESH
F32 = jnp.float32
BF16 = jnp.bfloat16


def attention_kernel(
    tp, ctx, rows,
    q_in, k_in, v_in, g_in,
    o_out, dq_out, dk_out, dv_out,
    qs, kx, vx, gs, kt, vt, scores, scores_too, ex, ot, rl, acc_k, acc_v, dlog,
    o_buf, dq_buf, dk_buf, dv_buf, halo_out, halo_in,
    in_send, in_recv, out_send, out_recv, halo_send, halo_recv, own_in, own_out,
):
    me = lax.axis_index("tp")
    place = lax.axis_index("ctx")
    ahead, behind = lax.rem(place + 1, ctx), lax.rem(place + ctx - 1, ctx)
    shard = rows * tp
    blocks = shard // rows
    span = WINDOW + rows
    halo_blocks = WINDOW // rows
    wide = GROUP * HEAD

    def at(i, size=rows):
        return pl.ds(pl.multiple_of(i * rows, rows), size)

    def columns(i, width):
        return pl.ds(pl.multiple_of(i * width, width), width)

    barrier = pltpu.get_barrier_semaphore()
    for n in range(1, tp):
        pl.semaphore_signal(barrier, inc=1, device_id={"tp": lax.rem(me + n, tp)}, device_id_type=MESH)
    pl.semaphore_signal(barrier, inc=1, device_id={"ctx": ahead}, device_id_type=MESH)
    pl.semaphore_signal(barrier, inc=1, device_id={"ctx": behind}, device_id_type=MESH)
    pl.semaphore_wait(barrier, tp + 1)

    incoming = (
        (k_in, kx, HEAD, halo_blocks),
        (v_in, vx, HEAD, halo_blocks),
        (q_in, qs, wide, 0),
        (g_in, gs, wide, 0),
    )

    def in_copy(i, owner, peer):
        source, target, width, first = incoming[i]
        return pltpu.make_async_remote_copy(
            src_ref=source.at[:, columns(peer, width)],
            dst_ref=target.at[at(first + owner), :],
            send_sem=in_send.at[i, peer],
            recv_sem=in_recv.at[i, owner],
            device_id={"tp": peer},
            device_id_type=MESH,
        )

    def own_copy(i):
        source, target, width, first = incoming[i]
        return pltpu.make_async_copy(
            source.at[:, columns(me, width)], target.at[at(first + me), :], own_in.at[i]
        )

    side = math.isqrt(tp)
    x, y = lax.rem(me, side), me // side
    core = lax.rem(place, 2)

    def partner(dx, dy):
        dx = jnp.where(core == 0, dx, side - dx)
        dy = jnp.where(core == 0, dy, side - dy)
        return lax.rem(y + dy, side) * side + lax.rem(x + dx, side)

    far = sorted(
        ((dx, dy) for dx in range(side) for dy in range(side) if dx or dy),
        key=lambda d: -(min(d[0], side - d[0]) + min(d[1], side - d[1])),
    )
    partners = [partner(dx, dy) for dx, dy in far]

    def nth_partner(n):
        peer = partners[0]
        for i in range(1, tp - 1):
            peer = jnp.where(n == i, partners[i], peer)
        return peer

    def send(i):
        for peer in partners:
            in_copy(i, me, peer).start()

    def sent(i):
        for peer in partners:
            in_copy(i, me, peer).wait_send()

    for i in FIRST:
        send(i)
    for i in range(4):
        own_copy(i).start()

    def arrived(i):
        def wait(n, _):
            in_copy(i, lax.rem(me + n, tp), me).wait_recv()
            return 0
        lax.fori_loop(1, tp, wait, 0)
        own_copy(i).wait()

    def arrived_block(i, b):
        @pl.when(b != me)
        def _():
            in_copy(i, b, me).wait_recv()

        @pl.when(b == me)
        def _():
            own_copy(i).wait()

    acc_k[...] = jnp.zeros_like(acc_k)
    acc_v[...] = jnp.zeros_like(acc_v)

    def halo_copy(i, source, target, where):
        return pltpu.make_async_remote_copy(
            src_ref=source, dst_ref=target, send_sem=halo_send.at[i], recv_sem=halo_recv.at[i],
            device_id={"ctx": where}, device_id_type=MESH,
        )

    halo_k = halo_copy(0, kx.at[pl.ds(shard, WINDOW), :], kx.at[pl.ds(0, WINDOW), :], ahead)
    halo_v = halo_copy(1, vx.at[pl.ds(shard, WINDOW), :], vx.at[pl.ds(0, WINDOW), :], ahead)
    halo_dk = halo_copy(2, halo_out.at[0], halo_in.at[0], behind)
    halo_dv = halo_copy(3, halo_out.at[1], halo_in.at[1], behind)

    def turn(source, target, first, count):
        def step(n, _):
            part = at(first + 4 * n, 4 * rows)
            target[:, part] = source[part, :].T
            return 0
        lax.fori_loop(0, count // 4, step, 0)

    arrived(0)
    halo_k.start()
    arrived(1)
    halo_v.start()
    turn(kx, kt, halo_blocks, blocks)
    turn(vx, vt, halo_blocks, blocks)
    sent(0)
    sent(1)
    for peer in partners[:EARLY]:
        in_copy(2, me, peer).wait_send()
    send(3)
    halo_k.wait_recv()
    turn(kx, kt, 0, halo_blocks)
    halo_v.wait_recv()
    turn(vx, vt, 0, halo_blocks)

    row_of = lax.broadcasted_iota(jnp.int32, (rows, wide), 0)
    col_of = lax.rem(lax.broadcasted_iota(jnp.int32, (rows, wide), 1), rows)
    causal = row_of <= col_of

    outgoing = (
        (o_buf, o_out, wide), (dq_buf, dq_out, wide), (dk_buf, dk_out, HEAD), (dv_buf, dv_out, HEAD),
    )

    def out_copy(i, owner, peer):
        source, target, width = outgoing[i]
        return pltpu.make_async_remote_copy(
            src_ref=source.at[peer],
            dst_ref=target.at[:, columns(owner, width)],
            send_sem=out_send.at[i, peer],
            recv_sem=out_recv.at[i, owner],
            device_id={"tp": peer},
            device_id_type=MESH,
        )

    def keep_copy(i):
        source, target, width = outgoing[i]
        return pltpu.make_async_copy(source.at[me], target.at[:, columns(me, width)], own_out.at[i])

    def deliver(i, b):
        @pl.when(b != me)
        def _():
            out_copy(i, me, b).start()

        @pl.when(b == me)
        def _():
            keep_copy(i).start()

    def stacked(ref, b):
        block = ref[at(b), :]
        return jnp.concatenate([block[:, :HEAD], block[:, HEAD:]], axis=0)

    def unstacked(t):
        return jnp.concatenate([t[:, :rows].T, t[:, rows:].T], axis=1)

    def fold(op, x):
        return op(x.reshape(rows // 8, 8, wide), axis=0)

    nt = (((1,), (1,)), ((), ()))
    chunks = WINDOW // rows

    def forward(b, scores):
        query = stacked(qs, b)
        scores[...] = lax.dot_general(kx[at(b, span), :], query, nt, preferred_element_type=F32)
        present = [jnp.logical_or(place > 0, j + b >= halo_blocks) for j in range(chunks)]
        diagonal = scores[pl.ds(WINDOW, rows), :]
        scores[pl.ds(0, rows), :] = jnp.where(
            causal, diagonal, jnp.where(present[0], scores[pl.ds(0, rows), :], -FAR)
        )
        top = fold(jnp.max, scores[pl.ds(0, rows), :])
        for j in range(1, chunks):
            part = fold(jnp.max, scores[pl.ds(j * rows, rows), :])
            top = jnp.maximum(top, jnp.where(present[j], part, -FAR))
        shift = jnp.max(top, axis=0, keepdims=True) * EXP_SCALE
        total = jnp.zeros((8, wide), F32)
        for j in range(chunks):
            by = shift if j == 0 else jnp.where(present[j], shift, FAR)
            e = jnp.exp2(scores[pl.ds(j * rows, rows), :] * EXP_SCALE - by)
            total = total + fold(jnp.sum, e)
            if j == 0:
                ex[b, pl.ds(0, rows), :] = jnp.where(causal, 0.0, e).astype(BF16)
                ex[b, pl.ds(WINDOW, rows), :] = jnp.where(causal, e, 0.0).astype(BF16)
            else:
                ex[b, pl.ds(j * rows, rows), :] = e.astype(BF16)
        inverse = 1.0 / jnp.sum(total, axis=0, keepdims=True)
        rl[b] = inverse
        out = jnp.dot(vt[:, at(b, span)], ex[b], preferred_element_type=F32) * inverse
        out = out.astype(BF16)
        ot[b] = out
        o_buf[b] = unstacked(out)

    def backward(b):
        arrived_block(3, b)
        query = stacked(qs, b)
        grad_t = (stacked(gs, b).astype(F32).T * rl[b]).astype(BF16)
        delta = jnp.sum(grad_t.astype(F32) * ot[b].astype(F32), axis=0, keepdims=True)
        grad = grad_t.T
        scores[...] = jnp.dot(vx[at(b, span), :], grad_t, preferred_element_type=F32)
        first = jnp.where(causal, scores[pl.ds(WINDOW, rows), :], scores[pl.ds(0, rows), :])
        e = ex[b, pl.ds(0, rows), :].astype(F32) + ex[b, pl.ds(WINDOW, rows), :].astype(F32)
        d = e * (first - delta)
        dlog[pl.ds(0, rows), :] = jnp.where(causal, 0.0, d).astype(BF16)
        dlog[pl.ds(WINDOW, rows), :] = jnp.where(causal, d, 0.0).astype(BF16)
        for j in range(1, chunks):
            part = pl.ds(j * rows, rows)
            dlog[part, :] = (ex[b, part, :].astype(F32) * (scores[part, :] - delta)).astype(BF16)
        window = at(b, span)
        acc_v[window, :] += jnp.dot(ex[b], grad, preferred_element_type=F32)
        acc_k[window, :] += jnp.dot(dlog[...], query, preferred_element_type=F32)
        dq_t = jnp.dot(kt[:, window], dlog[...], preferred_element_type=F32) * SCALE
        dq_buf[b] = unstacked(dq_t.astype(BF16))
        deliver(1, b)

    half = blocks // 2

    def over(base, count, work):
        def step(n, _):
            high = count // side
            dx = lax.rem(2 + lax.rem(n, side), side)
            dy = lax.rem(high // 2 + n // side, high)
            bx = lax.rem(x + jnp.where(core == 0, dx, side - dx), side)
            by = lax.rem(y + jnp.where(core == 0, dy, high - dy), high)
            work(base + by * side + bx)
            return 0
        lax.fori_loop(0, count, step, 0)

    def front(n, _):
        pair = (nth_partner(2 * n), jnp.where(n == tp // 2 - 1, me, nth_partner(2 * n + 1)))
        for b in pair:
            arrived_block(2, b)
        forward(pair[0], scores)
        forward(pair[1], scores_too)
        for b in pair:
            deliver(0, b)
        return 0

    lax.fori_loop(0, tp // 2, front, 0)
    over(0, half, backward)

    def pack(n, _):
        halo_out[0, at(n), :] = (acc_k[at(n), :] * SCALE).astype(BF16)
        halo_out[1, at(n), :] = acc_v[at(n), :].astype(BF16)
        return 0
    lax.fori_loop(0, halo_blocks, pack, 0)
    halo_dk.start()
    halo_dv.start()
    over(half, half, backward)

    def finish(b, late):
        own = at(b + halo_blocks)
        dk, dv = acc_k[own, :] * SCALE, acc_v[own, :]
        if late:
            more = at(b - (blocks - halo_blocks))
            dk += halo_in[0, more, :].astype(F32)
            dv += halo_in[1, more, :].astype(F32)
        dk_buf[b] = dk.astype(BF16)
        deliver(2, b)
        dv_buf[b] = dv.astype(BF16)
        deliver(3, b)

    over(0, half, functools.partial(finish, late=False))
    halo_dk.wait_recv()
    halo_dv.wait_recv()
    over(half, half, functools.partial(finish, late=True))

    for i in range(4):
        def wait(n, _, i=i):
            peer = lax.rem(me + n, tp)
            out_copy(i, me, peer).wait_send()
            out_copy(i, peer, me).wait_recv()
            return 0
        lax.fori_loop(1, tp, wait, 0)
        keep_copy(i).wait()
    for peer in partners[EARLY:]:
        in_copy(2, me, peer).wait_send()
    sent(3)
    for copy in (halo_k, halo_v, halo_dk, halo_dv):
        copy.wait_send()


def solution(mesh):
    tp, ctx = mesh.shape["tp"], mesh.shape["ctx"]

    def on_device(queries, keys, values, output_gradient):
        rows = queries.shape[0]
        shard = rows * tp
        wide = GROUP * HEAD
        span = WINDOW + rows
        hbm = pl.BlockSpec(memory_space=pl.ANY)
        vmem = pl.BlockSpec(memory_space=pltpu.VMEM)
        dma = pltpu.SemaphoreType.DMA
        results = pl.pallas_call(
            functools.partial(attention_kernel, tp, ctx, rows),
            out_shape=[pltpu.VMEM(a.shape, BF16) for a in (queries, queries, keys, keys)],
            in_specs=[hbm] * 4,
            out_specs=[vmem] * 4,
            scratch_shapes=[
                pltpu.VMEM((shard, wide), BF16),
                pltpu.VMEM((WINDOW + shard, HEAD), BF16),
                pltpu.VMEM((WINDOW + shard, HEAD), BF16),
                pltpu.VMEM((shard, wide), BF16),
                pltpu.VMEM((HEAD, WINDOW + shard), BF16),
                pltpu.VMEM((HEAD, WINDOW + shard), BF16),
                pltpu.VMEM((span, wide), F32),
                pltpu.VMEM((span, wide), F32),
                pltpu.VMEM((tp, span, wide), BF16),
                pltpu.VMEM((tp, HEAD, wide), BF16),
                pltpu.VMEM((tp, 1, wide), F32),
                pltpu.VMEM((WINDOW + shard, HEAD), F32),
                pltpu.VMEM((WINDOW + shard, HEAD), F32),
                pltpu.VMEM((span, wide), BF16),
                pltpu.VMEM((tp, rows, wide), BF16),
                pltpu.VMEM((tp, rows, wide), BF16),
                pltpu.VMEM((tp, rows, HEAD), BF16),
                pltpu.VMEM((tp, rows, HEAD), BF16),
                pltpu.VMEM((2, WINDOW, HEAD), BF16),
                pltpu.VMEM((2, WINDOW, HEAD), BF16),
                dma((4, tp)), dma((4, tp)), dma((4, tp)), dma((4, tp)),
                dma((4,)), dma((4,)), dma((4,)), dma((4,)),
            ],
            compiler_params=pltpu.CompilerParams(
                collective_id=0, has_side_effects=True, vmem_limit_bytes=60 << 20
            ),
        )(queries, keys, values, output_gradient)
        return results

    spec = P(("ctx", "tp"), None)
    return jax.shard_map(
        on_device, mesh=mesh, in_specs=(spec,) * 4, out_specs=(spec,) * 4, check_vma=False
    )
```

```python
import functools
import math

import jax
import jax.numpy as jnp
from jax import lax
from jax.experimental import pallas as pl
from jax.experimental.pallas import tpu as pltpu
from jax.sharding import PartitionSpec as P

HEAD = 128
GROUP = 2
WINDOW = 1024
QSCALE = 168
SCALE = QSCALE ** (-0.5)
EXP_SCALE = SCALE * math.log2(math.e)
FAR = 1e30
FIRST = (0, 1, 2)
EARLY = 10
MESH = pl.DeviceIdType.MESH
F32 = jnp.float32
BF16 = jnp.bfloat16


def attention_kernel(
    tp, ctx, rows,
    q_in, k_in, v_in, g_in,
    o_out, dq_out, dk_out, dv_out,
    qs, kx, vx, gs, kt, vt, scores, scores_too, ex, ot, rl, acc_k, acc_v, dlog, dlog_too,
    o_buf, dq_buf, dk_buf, dv_buf, halo_out, halo_in,
    in_send, in_recv, out_send, out_recv, halo_send, halo_recv, own_in, own_out,
):
    me = lax.axis_index("tp")
    place = lax.axis_index("ctx")
    ahead, behind = lax.rem(place + 1, ctx), lax.rem(place + ctx - 1, ctx)
    shard = rows * tp
    blocks = shard // rows
    span = WINDOW + rows
    halo_blocks = WINDOW // rows
    wide = GROUP * HEAD

    def at(i, size=rows):
        return pl.ds(pl.multiple_of(i * rows, rows), size)

    def columns(i, width):
        return pl.ds(pl.multiple_of(i * width, width), width)

    barrier = pltpu.get_barrier_semaphore()
    for n in range(1, tp):
        pl.semaphore_signal(barrier, inc=1, device_id={"tp": lax.rem(me + n, tp)}, device_id_type=MESH)
    pl.semaphore_signal(barrier, inc=1, device_id={"ctx": ahead}, device_id_type=MESH)
    pl.semaphore_signal(barrier, inc=1, device_id={"ctx": behind}, device_id_type=MESH)
    pl.semaphore_wait(barrier, tp + 1)

    incoming = (
        (k_in, kx, HEAD, halo_blocks),
        (v_in, vx, HEAD, halo_blocks),
        (q_in, qs, wide, 0),
        (g_in, gs, wide, 0),
    )

    def in_copy(i, owner, peer):
        source, target, width, first = incoming[i]
        return pltpu.make_async_remote_copy(
            src_ref=source.at[:, columns(peer, width)],
            dst_ref=target.at[at(first + owner), :],
            send_sem=in_send.at[i, peer],
            recv_sem=in_recv.at[i, owner],
            device_id={"tp": peer},
            device_id_type=MESH,
        )

    def own_copy(i):
        source, target, width, first = incoming[i]
        return pltpu.make_async_copy(
            source.at[:, columns(me, width)], target.at[at(first + me), :], own_in.at[i]
        )

    side = math.isqrt(tp)
    x, y = lax.rem(me, side), me // side
    core = lax.rem(place, 2)

    def partner(dx, dy):
        dx = jnp.where(core == 0, dx, side - dx)
        dy = jnp.where(core == 0, dy, side - dy)
        return lax.rem(y + dy, side) * side + lax.rem(x + dx, side)

    far = sorted(
        ((dx, dy) for dx in range(side) for dy in range(side) if dx or dy),
        key=lambda d: -(min(d[0], side - d[0]) + min(d[1], side - d[1])),
    )
    partners = [partner(dx, dy) for dx, dy in far]

    def nth_partner(n):
        peer = partners[0]
        for i in range(1, tp - 1):
            peer = jnp.where(n == i, partners[i], peer)
        return peer

    def send(i):
        for peer in partners:
            in_copy(i, me, peer).start()

    def sent(i):
        for peer in partners:
            in_copy(i, me, peer).wait_send()

    for i in FIRST:
        send(i)
    for i in range(4):
        own_copy(i).start()

    def arrived(i):
        def wait(n, _):
            in_copy(i, lax.rem(me + n, tp), me).wait_recv()
            return 0
        lax.fori_loop(1, tp, wait, 0)
        own_copy(i).wait()

    def arrived_block(i, b):
        @pl.when(b != me)
        def _():
            in_copy(i, b, me).wait_recv()

        @pl.when(b == me)
        def _():
            own_copy(i).wait()

    acc_k[...] = jnp.zeros_like(acc_k)
    acc_v[...] = jnp.zeros_like(acc_v)

    def halo_copy(i, source, target, where):
        return pltpu.make_async_remote_copy(
            src_ref=source, dst_ref=target, send_sem=halo_send.at[i], recv_sem=halo_recv.at[i],
            device_id={"ctx": where}, device_id_type=MESH,
        )

    halo_k = halo_copy(0, kx.at[pl.ds(shard, WINDOW), :], kx.at[pl.ds(0, WINDOW), :], ahead)
    halo_v = halo_copy(1, vx.at[pl.ds(shard, WINDOW), :], vx.at[pl.ds(0, WINDOW), :], ahead)
    halo_dk = halo_copy(2, halo_out.at[0], halo_in.at[0], behind)
    halo_dv = halo_copy(3, halo_out.at[1], halo_in.at[1], behind)

    def turn(source, target, first, count):
        def step(n, _):
            part = at(first + 4 * n, 4 * rows)
            target[:, part] = source[part, :].T
            return 0
        lax.fori_loop(0, count // 4, step, 0)

    arrived(0)
    halo_k.start()
    arrived(1)
    halo_v.start()
    turn(kx, kt, halo_blocks, blocks)
    turn(vx, vt, halo_blocks, blocks)
    sent(0)
    sent(1)
    for peer in partners[:EARLY]:
        in_copy(2, me, peer).wait_send()
    send(3)
    halo_k.wait_recv()
    turn(kx, kt, 0, halo_blocks)
    halo_v.wait_recv()
    turn(vx, vt, 0, halo_blocks)

    row_of = lax.broadcasted_iota(jnp.int32, (rows, wide), 0)
    col_of = lax.rem(lax.broadcasted_iota(jnp.int32, (rows, wide), 1), rows)
    causal = row_of <= col_of

    outgoing = (
        (o_buf, o_out, wide), (dq_buf, dq_out, wide), (dk_buf, dk_out, HEAD), (dv_buf, dv_out, HEAD),
    )

    def out_copy(i, owner, peer):
        source, target, width = outgoing[i]
        return pltpu.make_async_remote_copy(
            src_ref=source.at[peer],
            dst_ref=target.at[:, columns(owner, width)],
            send_sem=out_send.at[i, peer],
            recv_sem=out_recv.at[i, owner],
            device_id={"tp": peer},
            device_id_type=MESH,
        )

    def keep_copy(i):
        source, target, width = outgoing[i]
        return pltpu.make_async_copy(source.at[me], target.at[:, columns(me, width)], own_out.at[i])

    def deliver(i, b):
        @pl.when(b != me)
        def _():
            out_copy(i, me, b).start()

        @pl.when(b == me)
        def _():
            keep_copy(i).start()

    def stacked(ref, b):
        block = ref[at(b), :]
        return jnp.concatenate([block[:, :HEAD], block[:, HEAD:]], axis=0)

    def unstacked(t):
        return jnp.concatenate([t[:, :rows].T, t[:, rows:].T], axis=1)

    def fold(op, x):
        return op(x.reshape(rows // 8, 8, wide), axis=0)

    nt = (((1,), (1,)), ((), ()))
    chunks = WINDOW // rows

    def forward(b, scores):
        query = stacked(qs, b)
        scores[...] = lax.dot_general(kx[at(b, span), :], query, nt, preferred_element_type=F32)
        present = [jnp.logical_or(place > 0, j + b >= halo_blocks) for j in range(chunks)]
        diagonal = scores[pl.ds(WINDOW, rows), :]
        scores[pl.ds(0, rows), :] = jnp.where(
            causal, diagonal, jnp.where(present[0], scores[pl.ds(0, rows), :], -FAR)
        )
        top = fold(jnp.max, scores[pl.ds(0, rows), :])
        for j in range(1, chunks):
            part = fold(jnp.max, scores[pl.ds(j * rows, rows), :])
            top = jnp.maximum(top, jnp.where(present[j], part, -FAR))
        shift = jnp.max(top, axis=0, keepdims=True) * EXP_SCALE
        total = jnp.zeros((8, wide), F32)
        for j in range(chunks):
            by = shift if j == 0 else jnp.where(present[j], shift, FAR)
            e = jnp.exp2(scores[pl.ds(j * rows, rows), :] * EXP_SCALE - by)
            total = total + fold(jnp.sum, e)
            if j == 0:
                ex[b, pl.ds(0, rows), :] = jnp.where(causal, 0.0, e).astype(BF16)
                ex[b, pl.ds(WINDOW, rows), :] = jnp.where(causal, e, 0.0).astype(BF16)
            else:
                ex[b, pl.ds(j * rows, rows), :] = e.astype(BF16)
        inverse = 1.0 / jnp.sum(total, axis=0, keepdims=True)
        rl[b] = inverse
        out = jnp.dot(vt[:, at(b, span)], ex[b], preferred_element_type=F32) * inverse
        out = out.astype(BF16)
        ot[b] = out
        o_buf[b] = unstacked(out)

    def backward(b, scores, dlog):
        query = stacked(qs, b)
        grad_t = (stacked(gs, b).astype(F32).T * rl[b]).astype(BF16)
        delta = jnp.sum(grad_t.astype(F32) * ot[b].astype(F32), axis=0, keepdims=True)
        grad = grad_t.T
        scores[...] = jnp.dot(vx[at(b, span), :], grad_t, preferred_element_type=F32)
        first = jnp.where(causal, scores[pl.ds(WINDOW, rows), :], scores[pl.ds(0, rows), :])
        e = ex[b, pl.ds(0, rows), :].astype(F32) + ex[b, pl.ds(WINDOW, rows), :].astype(F32)
        d = e * (first - delta)
        dlog[pl.ds(0, rows), :] = jnp.where(causal, 0.0, d).astype(BF16)
        dlog[pl.ds(WINDOW, rows), :] = jnp.where(causal, d, 0.0).astype(BF16)
        for j in range(1, chunks):
            part = pl.ds(j * rows, rows)
            dlog[part, :] = (ex[b, part, :].astype(F32) * (scores[part, :] - delta)).astype(BF16)
        window = at(b, span)
        acc_v[window, :] += jnp.dot(ex[b], grad, preferred_element_type=F32)
        acc_k[window, :] += jnp.dot(dlog[...], query, preferred_element_type=F32)
        dq_t = jnp.dot(kt[:, window], dlog[...], preferred_element_type=F32) * SCALE
        dq_buf[b] = unstacked(dq_t.astype(BF16))

    half = blocks // 2

    def over(base, count, work, many=1):
        def place_of(n):
            high = count // side
            dx = lax.rem(2 + lax.rem(n, side), side)
            dy = lax.rem(high // 2 + n // side, high)
            bx = lax.rem(x + jnp.where(core == 0, dx, side - dx), side)
            by = lax.rem(y + jnp.where(core == 0, dy, high - dy), high)
            return base + by * side + bx

        def step(n, _):
            work(*[place_of(many * n + i) for i in range(many)])
            return 0
        lax.fori_loop(0, count // many, step, 0)

    def back(*pair):
        for b in pair:
            arrived_block(3, b)
        backward(pair[0], scores, dlog)
        backward(pair[1], scores_too, dlog_too)
        for b in pair:
            deliver(1, b)

    def front(n, _):
        pair = (nth_partner(2 * n), jnp.where(n == tp // 2 - 1, me, nth_partner(2 * n + 1)))
        for b in pair:
            arrived_block(2, b)
        forward(pair[0], scores)
        forward(pair[1], scores_too)
        for b in pair:
            deliver(0, b)
        return 0

    lax.fori_loop(0, tp // 2, front, 0)
    over(0, half, back, 2)

    def pack(n, _):
        halo_out[0, at(n), :] = (acc_k[at(n), :] * SCALE).astype(BF16)
        halo_out[1, at(n), :] = acc_v[at(n), :].astype(BF16)
        return 0
    lax.fori_loop(0, halo_blocks, pack, 0)
    halo_dk.start()
    halo_dv.start()
    over(half, half, back, 2)

    def finish(b, late):
        own = at(b + halo_blocks)
        dk, dv = acc_k[own, :] * SCALE, acc_v[own, :]
        if late:
            more = at(b - (blocks - halo_blocks))
            dk += halo_in[0, more, :].astype(F32)
            dv += halo_in[1, more, :].astype(F32)
        dk_buf[b] = dk.astype(BF16)
        deliver(2, b)
        dv_buf[b] = dv.astype(BF16)
        deliver(3, b)

    over(0, half, functools.partial(finish, late=False))
    halo_dk.wait_recv()
    halo_dv.wait_recv()
    over(half, half, functools.partial(finish, late=True))

    for i in range(4):
        def wait(n, _, i=i):
            peer = lax.rem(me + n, tp)
            out_copy(i, me, peer).wait_send()
            out_copy(i, peer, me).wait_recv()
            return 0
        lax.fori_loop(1, tp, wait, 0)
        keep_copy(i).wait()
    for peer in partners[EARLY:]:
        in_copy(2, me, peer).wait_send()
    sent(3)
    for copy in (halo_k, halo_v, halo_dk, halo_dv):
        copy.wait_send()


def solution(mesh):
    tp, ctx = mesh.shape["tp"], mesh.shape["ctx"]

    def on_device(queries, keys, values, output_gradient):
        rows = queries.shape[0]
        shard = rows * tp
        wide = GROUP * HEAD
        span = WINDOW + rows
        hbm = pl.BlockSpec(memory_space=pl.ANY)
        vmem = pl.BlockSpec(memory_space=pltpu.VMEM)
        dma = pltpu.SemaphoreType.DMA
        results = pl.pallas_call(
            functools.partial(attention_kernel, tp, ctx, rows),
            out_shape=[pltpu.VMEM(a.shape, BF16) for a in (queries, queries, keys, keys)],
            in_specs=[hbm] * 4,
            out_specs=[vmem] * 4,
            scratch_shapes=[
                pltpu.VMEM((shard, wide), BF16),
                pltpu.VMEM((WINDOW + shard, HEAD), BF16),
                pltpu.VMEM((WINDOW + shard, HEAD), BF16),
                pltpu.VMEM((shard, wide), BF16),
                pltpu.VMEM((HEAD, WINDOW + shard), BF16),
                pltpu.VMEM((HEAD, WINDOW + shard), BF16),
                pltpu.VMEM((span, wide), F32),
                pltpu.VMEM((span, wide), F32),
                pltpu.VMEM((tp, span, wide), BF16),
                pltpu.VMEM((tp, HEAD, wide), BF16),
                pltpu.VMEM((tp, 1, wide), F32),
                pltpu.VMEM((WINDOW + shard, HEAD), F32),
                pltpu.VMEM((WINDOW + shard, HEAD), F32),
                pltpu.VMEM((span, wide), BF16),
                pltpu.VMEM((span, wide), BF16),
                pltpu.VMEM((tp, rows, wide), BF16),
                pltpu.VMEM((tp, rows, wide), BF16),
                pltpu.VMEM((tp, rows, HEAD), BF16),
                pltpu.VMEM((tp, rows, HEAD), BF16),
                pltpu.VMEM((2, WINDOW, HEAD), BF16),
                pltpu.VMEM((2, WINDOW, HEAD), BF16),
                dma((4, tp)), dma((4, tp)), dma((4, tp)), dma((4, tp)),
                dma((4,)), dma((4,)), dma((4,)), dma((4,)),
            ],
            compiler_params=pltpu.CompilerParams(
                collective_id=0, has_side_effects=True, vmem_limit_bytes=60 << 20
            ),
        )(queries, keys, values, output_gradient)
        return results

    spec = P(("ctx", "tp"), None)
    return jax.shard_map(
        on_device, mesh=mesh, in_specs=(spec,) * 4, out_specs=(spec,) * 4, check_vma=False
    )
```

```python
import functools
import math

import jax
import jax.numpy as jnp
from jax import lax
from jax.experimental import pallas as pl
from jax.experimental.pallas import tpu as pltpu
from jax.sharding import PartitionSpec as P

HEAD = 128
GROUP = 2
WINDOW = 1024
QSCALE = 168
SCALE = QSCALE ** (-0.5)
EXP_SCALE = SCALE * math.log2(math.e)
FAR = 1e30
FIRST = (0, 1, 2)
EARLY = 7
MESH = pl.DeviceIdType.MESH
F32 = jnp.float32
BF16 = jnp.bfloat16


def attention_kernel(
    tp, ctx, rows,
    q_in, k_in, v_in, g_in,
    o_out, dq_out, dk_out, dv_out,
    qs, kx, vx, gs, kt, vt, scores, scores_too, ex, ot, rl, acc_k, acc_v, dlog,
    o_buf, dq_buf, dk_buf, dv_buf, halo_out, halo_in,
    in_send, in_recv, out_send, out_recv, halo_send, halo_recv, own_in, own_out,
):
    me = lax.axis_index("tp")
    place = lax.axis_index("ctx")
    ahead, behind = lax.rem(place + 1, ctx), lax.rem(place + ctx - 1, ctx)
    shard = rows * tp
    blocks = shard // rows
    span = WINDOW + rows
    halo_blocks = WINDOW // rows
    wide = GROUP * HEAD

    def at(i, size=rows):
        return pl.ds(pl.multiple_of(i * rows, rows), size)

    def columns(i, width):
        return pl.ds(pl.multiple_of(i * width, width), width)

    barrier = pltpu.get_barrier_semaphore()
    for n in range(1, tp):
        pl.semaphore_signal(barrier, inc=1, device_id={"tp": lax.rem(me + n, tp)}, device_id_type=MESH)
    pl.semaphore_signal(barrier, inc=1, device_id={"ctx": ahead}, device_id_type=MESH)
    pl.semaphore_signal(barrier, inc=1, device_id={"ctx": behind}, device_id_type=MESH)
    pl.semaphore_wait(barrier, tp + 1)

    incoming = (
        (k_in, kx, HEAD, halo_blocks),
        (v_in, vx, HEAD, halo_blocks),
        (q_in, qs, wide, 0),
        (g_in, gs, wide, 0),
    )

    def in_copy(i, owner, peer):
        source, target, width, first = incoming[i]
        return pltpu.make_async_remote_copy(
            src_ref=source.at[:, columns(peer, width)],
            dst_ref=target.at[at(first + owner), :],
            send_sem=in_send.at[i, peer],
            recv_sem=in_recv.at[i, owner],
            device_id={"tp": peer},
            device_id_type=MESH,
        )

    def own_copy(i):
        source, target, width, first = incoming[i]
        return pltpu.make_async_copy(
            source.at[:, columns(me, width)], target.at[at(first + me), :], own_in.at[i]
        )

    side = math.isqrt(tp)
    x, y = lax.rem(me, side), me // side
    core = lax.rem(place, 2)

    def partner(dx, dy):
        dx = jnp.where(core == 0, dx, side - dx)
        dy = jnp.where(core == 0, dy, side - dy)
        return lax.rem(y + dy, side) * side + lax.rem(x + dx, side)

    far = sorted(
        ((dx, dy) for dx in range(side) for dy in range(side) if dx or dy),
        key=lambda d: -(min(d[0], side - d[0]) + min(d[1], side - d[1])),
    )
    partners = [partner(dx, dy) for dx, dy in far]

    def nth_partner(n):
        peer = partners[0]
        for i in range(1, tp - 1):
            peer = jnp.where(n == i, partners[i], peer)
        return peer

    def send(i):
        for peer in partners:
            in_copy(i, me, peer).start()

    def sent(i):
        for peer in partners:
            in_copy(i, me, peer).wait_send()

    for i in FIRST:
        send(i)
    for i in range(4):
        own_copy(i).start()

    def arrived(i):
        def wait(n, _):
            in_copy(i, lax.rem(me + n, tp), me).wait_recv()
            return 0
        lax.fori_loop(1, tp, wait, 0)
        own_copy(i).wait()

    def arrived_block(i, b):
        @pl.when(b != me)
        def _():
            in_copy(i, b, me).wait_recv()

        @pl.when(b == me)
        def _():
            own_copy(i).wait()

    acc_k[...] = jnp.zeros_like(acc_k)
    acc_v[...] = jnp.zeros_like(acc_v)

    def halo_copy(i, source, target, where):
        return pltpu.make_async_remote_copy(
            src_ref=source, dst_ref=target, send_sem=halo_send.at[i], recv_sem=halo_recv.at[i],
            device_id={"ctx": where}, device_id_type=MESH,
        )

    halo_k = halo_copy(0, kx.at[pl.ds(shard, WINDOW), :], kx.at[pl.ds(0, WINDOW), :], ahead)
    halo_v = halo_copy(1, vx.at[pl.ds(shard, WINDOW), :], vx.at[pl.ds(0, WINDOW), :], ahead)
    halo_dk = halo_copy(2, halo_out.at[0], halo_in.at[0], behind)
    halo_dv = halo_copy(3, halo_out.at[1], halo_in.at[1], behind)

    def turn(source, target, first, count):
        def step(n, _):
            part = at(first + 4 * n, 4 * rows)
            target[:, part] = source[part, :].T
            return 0
        lax.fori_loop(0, count // 4, step, 0)

    arrived(0)
    halo_k.start()
    arrived(1)
    halo_v.start()
    turn(kx, kt, halo_blocks, blocks)
    turn(vx, vt, halo_blocks, blocks)
    sent(0)
    sent(1)
    for peer in partners[:EARLY]:
        in_copy(2, me, peer).wait_send()
    send(3)
    halo_k.wait_recv()
    turn(kx, kt, 0, halo_blocks)
    halo_v.wait_recv()
    turn(vx, vt, 0, halo_blocks)

    row_of = lax.broadcasted_iota(jnp.int32, (rows, wide), 0)
    col_of = lax.rem(lax.broadcasted_iota(jnp.int32, (rows, wide), 1), rows)
    causal = row_of <= col_of

    outgoing = (
        (o_buf, o_out, wide), (dq_buf, dq_out, wide), (dk_buf, dk_out, HEAD), (dv_buf, dv_out, HEAD),
    )

    def out_copy(i, owner, peer):
        source, target, width = outgoing[i]
        return pltpu.make_async_remote_copy(
            src_ref=source.at[peer],
            dst_ref=target.at[:, columns(owner, width)],
            send_sem=out_send.at[i, peer],
            recv_sem=out_recv.at[i, owner],
            device_id={"tp": peer},
            device_id_type=MESH,
        )

    def keep_copy(i):
        source, target, width = outgoing[i]
        return pltpu.make_async_copy(source.at[me], target.at[:, columns(me, width)], own_out.at[i])

    def deliver(i, b):
        @pl.when(b != me)
        def _():
            out_copy(i, me, b).start()

        @pl.when(b == me)
        def _():
            keep_copy(i).start()

    def stacked(ref, b):
        block = ref[at(b), :]
        return jnp.concatenate([block[:, :HEAD], block[:, HEAD:]], axis=0)

    def unstacked(t):
        return jnp.concatenate([t[:, :rows].T, t[:, rows:].T], axis=1)

    def fold(op, x):
        return op(x.reshape(rows // 8, 8, wide), axis=0)

    nt = (((1,), (1,)), ((), ()))
    chunks = WINDOW // rows

    def forward(b, scores):
        query = stacked(qs, b)
        scores[...] = lax.dot_general(kx[at(b, span), :], query, nt, preferred_element_type=F32)
        present = [jnp.logical_or(place > 0, j + b >= halo_blocks) for j in range(chunks)]
        diagonal = scores[pl.ds(WINDOW, rows), :]
        scores[pl.ds(0, rows), :] = jnp.where(
            causal, diagonal, jnp.where(present[0], scores[pl.ds(0, rows), :], -FAR)
        )
        top = fold(jnp.max, scores[pl.ds(0, rows), :])
        for j in range(1, chunks):
            part = fold(jnp.max, scores[pl.ds(j * rows, rows), :])
            top = jnp.maximum(top, jnp.where(present[j], part, -FAR))
        shift = jnp.max(top, axis=0, keepdims=True) * EXP_SCALE
        total = jnp.zeros((8, wide), F32)
        for j in range(chunks):
            by = shift if j == 0 else jnp.where(present[j], shift, FAR)
            e = jnp.exp2(scores[pl.ds(j * rows, rows), :] * EXP_SCALE - by)
            total = total + fold(jnp.sum, e)
            if j == 0:
                ex[b, pl.ds(0, rows), :] = jnp.where(causal, 0.0, e).astype(BF16)
                ex[b, pl.ds(WINDOW, rows), :] = jnp.where(causal, e, 0.0).astype(BF16)
            else:
                ex[b, pl.ds(j * rows, rows), :] = e.astype(BF16)
        inverse = 1.0 / jnp.sum(total, axis=0, keepdims=True)
        rl[b] = inverse
        out = jnp.dot(vt[:, at(b, span)], ex[b], preferred_element_type=F32) * inverse
        out = out.astype(BF16)
        ot[b] = out
        o_buf[b] = unstacked(out)

    def backward(b):
        arrived_block(3, b)
        query = stacked(qs, b)
        grad_t = (stacked(gs, b).astype(F32).T * rl[b]).astype(BF16)
        delta = jnp.sum(grad_t.astype(F32) * ot[b].astype(F32), axis=0, keepdims=True)
        grad = grad_t.T
        scores[...] = jnp.dot(vx[at(b, span), :], grad_t, preferred_element_type=F32)
        first = jnp.where(causal, scores[pl.ds(WINDOW, rows), :], scores[pl.ds(0, rows), :])
        e = ex[b, pl.ds(0, rows), :].astype(F32) + ex[b, pl.ds(WINDOW, rows), :].astype(F32)
        d = e * (first - delta)
        dlog[pl.ds(0, rows), :] = jnp.where(causal, 0.0, d).astype(BF16)
        dlog[pl.ds(WINDOW, rows), :] = jnp.where(causal, d, 0.0).astype(BF16)
        for j in range(1, chunks):
            part = pl.ds(j * rows, rows)
            dlog[part, :] = (ex[b, part, :].astype(F32) * (scores[part, :] - delta)).astype(BF16)
        window = at(b, span)
        acc_v[window, :] += jnp.dot(ex[b], grad, preferred_element_type=F32)
        acc_k[window, :] += jnp.dot(dlog[...], query, preferred_element_type=F32)
        dq_t = jnp.dot(kt[:, window], dlog[...], preferred_element_type=F32) * SCALE
        dq_buf[b] = unstacked(dq_t.astype(BF16))
        deliver(1, b)

    half = blocks // 2

    def over(base, count, work):
        def step(n, _):
            high = count // side
            dx = lax.rem(2 + lax.rem(n, side), side)
            dy = lax.rem(high // 2 + n // side, high)
            bx = lax.rem(x + jnp.where(core == 0, dx, side - dx), side)
            by = lax.rem(y + jnp.where(core == 0, dy, high - dy), high)
            work(base + by * side + bx)
            return 0
        lax.fori_loop(0, count, step, 0)

    def front(n, _):
        pair = (nth_partner(2 * n), jnp.where(n == tp // 2 - 1, me, nth_partner(2 * n + 1)))
        for b in pair:
            arrived_block(2, b)
        forward(pair[0], scores)
        forward(pair[1], scores_too)
        for b in pair:
            deliver(0, b)
        return 0

    lax.fori_loop(0, tp // 2, front, 0)
    over(0, half, backward)

    def pack(n, _):
        halo_out[0, at(n), :] = (acc_k[at(n), :] * SCALE).astype(BF16)
        halo_out[1, at(n), :] = acc_v[at(n), :].astype(BF16)
        return 0
    lax.fori_loop(0, halo_blocks, pack, 0)
    halo_dk.start()
    halo_dv.start()
    over(half, half, backward)

    def finish(b, late):
        own = at(b + halo_blocks)
        dk, dv = acc_k[own, :] * SCALE, acc_v[own, :]
        if late:
            more = at(b - (blocks - halo_blocks))
            dk += halo_in[0, more, :].astype(F32)
            dv += halo_in[1, more, :].astype(F32)
        dk_buf[b] = dk.astype(BF16)
        deliver(2, b)
        dv_buf[b] = dv.astype(BF16)
        deliver(3, b)

    over(0, half, functools.partial(finish, late=False))
    halo_dk.wait_recv()
    halo_dv.wait_recv()
    over(half, half, functools.partial(finish, late=True))

    for i in range(4):
        def wait(n, _, i=i):
            peer = lax.rem(me + n, tp)
            out_copy(i, me, peer).wait_send()
            out_copy(i, peer, me).wait_recv()
            return 0
        lax.fori_loop(1, tp, wait, 0)
        keep_copy(i).wait()
    for peer in partners[EARLY:]:
        in_copy(2, me, peer).wait_send()
    sent(3)
    for copy in (halo_k, halo_v, halo_dk, halo_dv):
        copy.wait_send()


def solution(mesh):
    tp, ctx = mesh.shape["tp"], mesh.shape["ctx"]

    def on_device(queries, keys, values, output_gradient):
        rows = queries.shape[0]
        shard = rows * tp
        wide = GROUP * HEAD
        span = WINDOW + rows
        hbm = pl.BlockSpec(memory_space=pl.ANY)
        vmem = pl.BlockSpec(memory_space=pltpu.VMEM)
        dma = pltpu.SemaphoreType.DMA
        results = pl.pallas_call(
            functools.partial(attention_kernel, tp, ctx, rows),
            out_shape=[pltpu.VMEM(a.shape, BF16) for a in (queries, queries, keys, keys)],
            in_specs=[hbm] * 4,
            out_specs=[vmem] * 4,
            scratch_shapes=[
                pltpu.VMEM((shard, wide), BF16),
                pltpu.VMEM((WINDOW + shard, HEAD), BF16),
                pltpu.VMEM((WINDOW + shard, HEAD), BF16),
                pltpu.VMEM((shard, wide), BF16),
                pltpu.VMEM((HEAD, WINDOW + shard), BF16),
                pltpu.VMEM((HEAD, WINDOW + shard), BF16),
                pltpu.VMEM((span, wide), F32),
                pltpu.VMEM((span, wide), F32),
                pltpu.VMEM((tp, span, wide), BF16),
                pltpu.VMEM((tp, HEAD, wide), BF16),
                pltpu.VMEM((tp, 1, wide), F32),
                pltpu.VMEM((WINDOW + shard, HEAD), F32),
                pltpu.VMEM((WINDOW + shard, HEAD), F32),
                pltpu.VMEM((span, wide), BF16),
                pltpu.VMEM((tp, rows, wide), BF16),
                pltpu.VMEM((tp, rows, wide), BF16),
                pltpu.VMEM((tp, rows, HEAD), BF16),
                pltpu.VMEM((tp, rows, HEAD), BF16),
                pltpu.VMEM((2, WINDOW, HEAD), BF16),
                pltpu.VMEM((2, WINDOW, HEAD), BF16),
                dma((4, tp)), dma((4, tp)), dma((4, tp)), dma((4, tp)),
                dma((4,)), dma((4,)), dma((4,)), dma((4,)),
            ],
            compiler_params=pltpu.CompilerParams(
                collective_id=0, has_side_effects=True, vmem_limit_bytes=60 << 20
            ),
        )(queries, keys, values, output_gradient)
        return results

    spec = P(("ctx", "tp"), None)
    return jax.shard_map(
        on_device, mesh=mesh, in_specs=(spec,) * 4, out_specs=(spec,) * 4, check_vma=False
    )
```
